256 devices in a mesh: rep: 4 (over y), exp: 64 (over z, x, core).
Axes of the slice: x: 4, y: 4, z: 8, core: 2. Of those that a mesh axis runs over, the one named last changes fastest.
Arguments:
- hidden_states: bfloat16 [4096, 4096], P(('rep', 'exp')), may hold values from -6 to 6
- expert_ids: int32 [4096, 8], P(('rep', 'exp')), may hold values from 0 to 63, as said below
- route_weights: float32 [4096, 8], P(('rep', 'exp')), may hold values from 0.05 to 1
- w_gate: bfloat16 [64, 4096, 1536], P('exp', None, 'rep'), may hold values from -0.09375 to 0.09375
- w_up: bfloat16 [64, 4096, 1536], P('exp', None, 'rep'), may hold values from -0.09375 to 0.09375
- w_down: bfloat16 [64, 1536, 4096], P('exp', 'rep'), may hold values from -0.15625 to 0.15625
Outputs:
- moe_out: bfloat16 [4096, 4096], P(('rep', 'exp'))
The draws below stay inside these ranges and needn't reach their ends.
Inputs may be any that keep to these rules, and one draw needn't show every extreme that they name: `expert_ids`: each row names 8 different experts. One expert, the same for the whole array, is named by exactly 6 of the 16 rows held by each device (each device's block of 16 consecutive rows); every other expert is named by at most 2 rows of one device, and in every device's rows some expert other than that one reaches 2.
All inputs are finite; a program needn't handle non-finite values.
Results may differ from the reference program's by a relative error of at most 0.015.
Values may be sent and summed in bfloat16 or wider, within the bound.
A program may use at most 128 MiB of HBM per device.

```python
import jax
import jax.numpy as jnp
from jax import lax

D = 4096
FF = 1536
TOPK = 8
TOK_DEV = 16
EXPERTS = 64
TOKENS = 4096
HOT_ROWS = 6
N_REP = 4


def draw_expert_ids(key, part):
    blocks = TOKENS // TOK_DEV
    cold = EXPERTS - 1
    key_hot, key_rows, key_cold, key_roll = jax.random.split(key, 4)
    hot = jax.random.randint(key_hot, (), 0, EXPERTS)
    row_keys = jax.random.split(key_rows, blocks)
    order = jax.vmap(lambda k: jax.random.permutation(k, TOK_DEV))(row_keys)
    is_hot = (order < HOT_ROWS).astype(jnp.int32)
    cold_keys = jax.random.split(key_cold, blocks)
    cold_perm = jax.vmap(lambda k: jax.random.permutation(k, cold))(cold_keys)
    need = TOPK - is_hot
    first = jnp.cumsum(need, axis=1) - need
    column = jnp.arange(TOPK, dtype=jnp.int32)[None, None, :]
    cold_slot = (first[:, :, None] + column - is_hot[:, :, None]) % cold
    values = jnp.take_along_axis(cold_perm, cold_slot.reshape(blocks, TOK_DEV * TOPK), axis=1)
    values = values.reshape(blocks, TOK_DEV, TOPK)
    cold_id = values + (values >= hot).astype(jnp.int32)
    chosen = jnp.where((column == 0) & (is_hot[:, :, None] == 1), hot, cold_id)
    shift = jax.random.randint(key_roll, (blocks, TOK_DEV), 0, TOPK)
    rolled = (column + shift[:, :, None]) % TOPK
    chosen = jnp.take_along_axis(chosen, rolled, axis=2)
    return chosen.reshape(TOKENS, TOPK).astype(jnp.int32)


def steps_of(stream_key, shape, shards, least, high):
    def one(axis_at, blocks):
        heights = jax.random.uniform(jax.random.fold_in(jax.random.fold_in(stream_key, 6), axis_at), (blocks,), jnp.float32, least / len(shards), high / len(shards))
        return jnp.repeat(jnp.exp(heights), shape[axis_at] // blocks).reshape((-1,) + (1,) * (len(shape) - axis_at - 1))

    factor_of = one(*shards[0])
    for cut in shards[1:]:
        factor_of = factor_of * one(*cut)
    return factor_of


def normal_values(rng, dims, scale, reach, cuts=(), held_as=jnp.bfloat16):
    factor_of = steps_of(rng, dims, cuts, -0.22, 0.18) if cuts else 1.0
    entries = jax.random.normal(rng, dims, jnp.float32) * scale * factor_of
    return jnp.minimum(jnp.maximum(entries, -reach), reach).astype(held_as)


def setup_inputs(seed: int = 0) -> dict:
    arg_keys = jax.random.split(jax.random.key(seed), 7)
    return {
        "hidden_states": normal_values(arg_keys[0], (TOKENS, D), 1.0, 6.0, ((0, 256),)),
        "expert_ids": draw_expert_ids(jax.random.fold_in(arg_keys[6], 71), 0),
        "route_weights": jnp.clip(0.05 + 0.95 * jax.random.uniform(arg_keys[2], (TOKENS, TOPK), jnp.float32) ** steps_of(arg_keys[2], (TOKENS, TOPK), ((0, 256),), -0.2, 0.2), 0.05, 1.0),
        "w_gate": normal_values(arg_keys[3], (EXPERTS, D, FF), D ** -0.5, 0.09375, ((0, 64), (2, 4))),
        "w_up": normal_values(arg_keys[4], (EXPERTS, D, FF), D ** -0.5, 0.09375, ((0, 64), (2, 4))),
        "w_down": normal_values(arg_keys[5], (EXPERTS, FF, D), FF ** -0.5, 0.15625, ((0, 64), (1, 4))),
    }


block_rows = 256


def expert_block(row_block, gate_w, up_w, down_w):
    gate_value = jnp.dot(row_block, gate_w, preferred_element_type=jnp.float32)
    up_value = jnp.dot(row_block, up_w, preferred_element_type=jnp.float32)
    active = (jax.nn.silu(gate_value) * up_value).astype(jnp.bfloat16)
    group = active.shape[1] // N_REP
    summed = jnp.zeros((row_block.shape[0], down_w.shape[1]), jnp.float32)
    for group_index in range(N_REP):
        lower = group_index * group
        piece = jnp.dot(active[:, lower:lower + group], down_w[lower:lower + group], preferred_element_type=jnp.float32)
        rounded = lax.optimization_barrier(piece.astype(jnp.bfloat16))
        summed = summed + rounded.astype(jnp.float32)
    return summed.astype(jnp.bfloat16)


def reference(hidden_states, expert_ids, route_weights, w_gate, w_up, w_down):
    tokens, width = hidden_states.shape
    topk = expert_ids.shape[1]
    experts = w_gate.shape[0]
    flat_ids = expert_ids.reshape(-1).astype(jnp.int32)
    picks = flat_ids.shape[0]
    onehot = (flat_ids[:, None] == jnp.arange(experts, dtype=jnp.int32)[None, :]).astype(jnp.int32)
    counts = jnp.sum(onehot, axis=0)
    rank = jnp.sum((jnp.cumsum(onehot, axis=0) - onehot) * onehot, axis=1)
    padded = (counts + block_rows - 1) // block_rows * block_rows
    start = jnp.cumsum(padded) - padded
    row_pos = (start[flat_ids] + rank).astype(jnp.int32)
    blocks = picks // block_rows + experts + 1
    total_rows = blocks * block_rows
    owner = jnp.zeros((total_rows,), jnp.int32).at[row_pos].set(jnp.arange(picks, dtype=jnp.int32) // topk)
    block_start = jnp.arange(blocks, dtype=jnp.int32) * block_rows
    block_expert = (jnp.sum((start[None, :] <= block_start[:, None]).astype(jnp.int32), axis=1) - 1).astype(jnp.int32)

    def run_block(inputs):
        expert, owners = inputs
        row_block = jnp.take(hidden_states, owners, axis=0)
        return expert_block(row_block, w_gate[expert], w_up[expert], w_down[expert])

    outputs = lax.map(run_block, (block_expert, owner.reshape(blocks, block_rows)))
    flat_out = outputs.reshape(total_rows, width)
    norm_weights = route_weights / jnp.sum(route_weights, axis=1, keepdims=True)
    picked = jnp.take(flat_out, row_pos, axis=0).astype(jnp.float32).reshape(tokens, topk, width)
    return jnp.sum(picked * norm_weights[:, :, None], axis=1).astype(jnp.bfloat16)
```

```python
import functools

import jax
import jax.numpy as jnp
from jax import lax
from jax.experimental import pallas as pl
from jax.experimental.pallas import tpu as pltpu
from jax.sharding import PartitionSpec as P

MESH = pl.DeviceIdType.MESH
BF = jnp.bfloat16
F32 = jnp.float32

NZ, NX, NY, NC = 8, 4, 4, 2
CHUNKS = 4
NSEM = 64


def kernel(tok_ref, meta_ref, hot_ref, wg_hbm, wu_hbm, wd_hbm, out_ref,
           zt, mt, xs, xc_buf, xh, wgu, wd, acc, act, ry, hc, rx, rh, rr, tk, zr,
           sel, mcomb, send_sem, recv_sem, load_sem):
    y = lax.axis_index("rep")
    e = lax.axis_index("exp")
    z = e // 8
    xcore = lax.rem(e, 8)
    x = xcore // 2
    c = lax.rem(e, 2)
    width = tok_ref.shape[1]
    W = width // CHUNKS
    NT = W // 256

    def add(v, k, n):
        return lax.rem(v + (k + n), n)

    def dev_z(k):
        return {"rep": y, "exp": add(z, k, NZ) * 8 + xcore}

    def dev_x(k):
        return {"rep": y, "exp": z * 8 + add(x, k, NX) * 2 + c}

    def dev_y(k):
        return {"rep": add(y, k, NY), "exp": e}

    def dev_xc(k):
        return {"rep": y, "exp": z * 8 + lax.rem(xcore + k, 8)}

    dev_sib = {"rep": y, "exp": z * 8 + x * 2 + (1 - c)}

    loads = [
        pltpu.make_async_copy(wg_hbm.at[0], wgu.at[:, pl.ds(0, 384)], load_sem.at[0]),
        pltpu.make_async_copy(wu_hbm.at[0], wgu.at[:, pl.ds(384, 384)], load_sem.at[1]),
        pltpu.make_async_copy(wd_hbm.at[0], wd, load_sem.at[2]),
    ]
    for cp in loads:
        cp.start()

    barrier = pltpu.get_barrier_semaphore()
    partners = [dev_z(1), dev_z(-1), dev_y(1), dev_y(-1)] + [dev_xc(k) for k in range(1, 8)]
    for p in partners:
        pl.semaphore_signal(barrier, inc=1, device_id=p, device_id_type=MESH)

    for j in range(CHUNKS):
        zt[j, z] = tok_ref[:, pl.ds(j * W, W)]
    mt[z] = meta_ref[...]

    pl.semaphore_wait(barrier, len(partners))

    count = [0]
    pending = []
    copies = {}

    def send(key, src, dst, dev):
        i = count[0]
        count[0] += 1
        cp = pltpu.make_async_remote_copy(
            src_ref=src, dst_ref=dst, send_sem=send_sem.at[i], recv_sem=recv_sem.at[i],
            device_id=dev, device_id_type=MESH)
        cp.start()
        copies[key] = cp
        pending.append(key)

    def got(key):
        copies[key].wait_recv()

    def sent(match):
        for key in list(pending):
            if match(key):
                copies[key].wait_send()
                pending.remove(key)

    def hops(j):
        return (4, 3) if j % 2 == 0 else (3, 4)

    def zg_start(tag, at, j, s):
        plus, minus = hops(j)
        if s <= plus:
            slot = add(z, -(s - 1), NZ)
            send((tag, j, "p", s), at(slot), at(slot), dev_z(1))
        if s <= minus:
            slot = add(z, s - 1, NZ)
            send((tag, j, "m", s), at(slot), at(slot), dev_z(-1))

    def zg_wait(tag, j, s):
        plus, minus = hops(j)
        if s <= plus:
            got((tag, j, "p", s))
        if s <= minus:
            got((tag, j, "m", s))

    def g4_first(tag, j, at, me, dev):
        send((tag, j, "p1"), at(me, None), at(me, None), dev(1))
        send((tag, j, "m1"), at(me, None), at(me, None), dev(-1))

    def g4_second(tag, j, at, me, dev):
        left, right = add(me, -1, 4), add(me, 1, 4)
        got((tag, j, "p1"))
        send((tag, j, "p2"), at(left, 0), at(left, 0), dev(1))
        got((tag, j, "m1"))
        send((tag, j, "m2"), at(right, 1), at(right, 1), dev(-1))

    def g4_done(tag, j):
        got((tag, j, "p2"))
        got((tag, j, "m2"))

    def r4_first(tag, j, at, slot, me, dev):
        left, right, far = add(me, -1, 4), add(me, 1, 4), add(me, 2, 4)
        send((tag, j, 0), at(far, 0), slot(0), dev(1))
        send((tag, j, 2), at(far, 1), slot(2), dev(-1))
        send((tag, j, 1), at(right, 1), slot(1), dev(1))
        send((tag, j, 3), at(left, 0), slot(3), dev(-1))

    def summed(dst, *parts):
        total = parts[0][...].astype(F32)
        for part in parts[1:]:
            total = total + part[...].astype(F32)
        dst[...] = total.astype(BF)

    def tiles(dst, *parts):
        @pl.loop(0, NT)
        def _(n):
            cols = pl.ds(pl.multiple_of(n * 256, 256), 256)
            lead = (slice(None),) * (len(dst.shape) - 1)
            summed(dst.at[lead + (cols,)], *[p.at[lead + (cols,)] for p in parts])

    def r4_second(tag, j, at, slot, me, dev):
        left, right = add(me, -1, 4), add(me, 1, 4)
        got((tag, j, 0))
        tiles(at(right, 0), at(right, 0), slot(0))
        send((tag, j, 4), at(right, 0), slot(4), dev(1))
        got((tag, j, 2))
        tiles(at(left, 1), at(left, 1), slot(2))
        send((tag, j, 5), at(left, 1), slot(5), dev(-1))

    def r4_done(tag, j, at, slot, me):
        for k in (1, 3, 4, 5):
            got((tag, j, k))
        tiles(at(me, 0), at(me, 0), slot(3), slot(4))
        tiles(at(me, 1), at(me, 1), slot(1), slot(5))

    def cold_at(j):
        def at(i, half):
            return xc_buf.at[j, i] if half is None else xc_buf.at[j, i, pl.ds(4 * half, 4)]
        return at

    def hoty_at(j):
        def at(i, half):
            return xh.at[j, c, x, i] if half is None else xh.at[j, c, x, i, half]
        return at

    def hotx_at(j):
        def at(i, half):
            return xh.at[j, c, i] if half is None else xh.at[j, c, i, pl.ds(2 * half, 2)]
        return at

    def meta_done():
        both = mt[0]
        for k in range(1, NZ):
            both = both + mt[k]
        codes = both[0:8].astype(jnp.int32) - 1
        weights = both[8:16]
        row = lax.broadcasted_iota(jnp.int32, (128, 128), 0)
        want = ((row >> 1) & 7) * 512 + (z * 8 + (row >> 4)) * 8 + (row & 1)
        pick = jnp.zeros((128, 128), F32)
        comb = jnp.zeros((128, 128), F32)
        for k in range(8):
            hit = codes[k:k + 1, :] == want
            pick = pick + jnp.where(hit, 1.0, 0.0)
            comb = comb + jnp.where(hit, weights[k:k + 1, :], 0.0)
        sel[0:128, :] = pick.astype(BF)
        comb = comb.T
        high = comb.astype(BF)
        mcomb[0] = high
        mcomb[1] = (comb - high.astype(F32)).astype(BF)
        want = (row >> 2) * 512 + (row & 3) + 2
        masked = (codes >> 9) * 512 + (codes & 7)
        pick = jnp.zeros((128, 128), F32)
        comb = jnp.zeros((128, 128), F32)
        for k in range(8):
            hit = masked[k:k + 1, :] == want
            pick = pick + jnp.where(hit, 1.0, 0.0)
            comb = comb + jnp.where(hit, weights[k:k + 1, :], 0.0)
        sel[128:160, :] = pick[0:32, :].astype(BF)
        comb = comb.T
        high = comb.astype(BF)
        mcomb[2] = high
        mcomb[3] = (comb - high.astype(F32)).astype(BF)

    def d_zstart(j):
        zg_start("z", lambda s: zt.at[j, s], j, 1)
        if j == 0:
            zg_start("meta", lambda s: mt.at[s], 0, 1)

    def d_zstep(s, j):
        if j == 0:
            zg_wait("meta", 0, s - 1)
            zg_start("meta", lambda i: mt.at[i], 0, s)
        zg_wait("z", j, s - 1)
        zg_start("z", lambda i: zt.at[j, i], j, s)

    def d_select(j):
        if j == 0:
            zg_wait("meta", 0, 4)
            meta_done()
        zg_wait("z", j, 4)

        @pl.loop(0, NT)
        def _(n):
            cols = pl.ds(pl.multiple_of(n * 256, 256), 256)
            rows = jnp.dot(sel[...], zt[j, :, :, cols].reshape(128, 256), preferred_element_type=F32)
            xs[j, :, :, cols] = rows.astype(BF).reshape(10, 16, 256)

        for k in range(1, 8):
            send(("x", j, k), xs.at[j, lax.rem(xcore + k, 8)], xc_buf.at[j, y, xcore], dev_xc(k))
        xh[j, c, x, y] = xs[j, 8:10]
        g4_first("hy", j, hoty_at(j), y, dev_y)
        xc_buf[j, y, xcore] = xs[j, xcore]

    def d_hoty2(j):
        g4_second("hy", j, hoty_at(j), y, dev_y)

    def d_coldy1(j):
        for k in range(1, 8):
            got(("x", j, k))
        g4_first("cy", j, cold_at(j), y, dev_y)

    def d_hotx1(j):
        g4_done("hy", j)
        g4_first("hx", j, hotx_at(j), x, dev_x)

    def d_coldy2(j):
        g4_second("cy", j, cold_at(j), y, dev_y)

    def d_hotx2(j):
        g4_second("hx", j, hotx_at(j), x, dev_x)

    def gate_up(j, block, at, shape, first):
        @pl.loop(0, 3)
        def _(n):
            cols = pl.ds(pl.multiple_of(n * 256, 256), 256)
            part = jnp.dot(at[...].reshape(512, W), wgu[pl.ds(j * W, W), cols],
                           preferred_element_type=F32)
            if first:
                acc[block, :, cols] = part
            else:
                acc[block, :, cols] += part

    def d_coldmm(j):
        g4_done("cy", j)
        if j == 0:
            loads[0].wait()
            loads[1].wait()
        gate_up(j, 0, xc_buf.at[j], (4, 8, 16), j == 0)

    def d_core(j):
        g4_done("hx", j)
        send(("core", j), xh.at[j, c], xh.at[j, c], dev_sib)

    def d_hotmm(j):
        got(("core", j))
        gate_up(j, 1, xh.at[j, 0], (4, 4, 2, 16), j == 0)
        gate_up(j, 2, xh.at[j, 1], (4, 4, 2, 16), j == 0)

    def activate(block, masked):
        @pl.loop(0, 8)
        def _(i):
            rows = pl.ds(pl.multiple_of(i * 64, 64), 64)
            gate = acc[block, rows, 0:384]
            up = acc[block, rows, 384:768]
            value = gate / (1.0 + jnp.exp(-gate)) * up
            if masked:
                value = jnp.where(hot_ref[0:1, 0:1] > 0.5, value, 0.0)
            act[block, rows, :] = value.astype(BF)

    def down(j, block, at, shape):
        @pl.loop(0, NT)
        def _(n):
            cols = pl.ds(pl.multiple_of(n * 256, 256), 256)
            wcols = pl.ds(pl.multiple_of(j * W + n * 256, 256), 256)
            part = jnp.dot(act[block], wd[:, wcols], preferred_element_type=F32)
            at[(slice(None),) * len(shape) + (cols,)] = part.astype(BF).reshape(shape + (256,))

    def silu_cold():
        loads[2].wait()
        activate(0, False)

    def silu_hot():
        activate(1, True)
        activate(2, True)

    def ry_at(j):
        return lambda k: ry.at[j, k]

    def rx_at(j):
        return lambda k: rx.at[j, k]

    def rh_at(j):
        return lambda k: rh.at[j, k]

    def e_down(j):
        sent(lambda key: key[0] == "cy" and key[1] == j)
        down(j, 0, xc_buf.at[j], (4, 8, 16))
        r4_first("ry", j, cold_at(j), ry_at(j), y, dev_y)

    def e_second(j):
        r4_second("ry", j, cold_at(j), ry_at(j), y, dev_y)

    def e_return(j):
        r4_done("ry", j, cold_at(j), ry_at(j), y)
        for k in range(1, 8):
            send(("back", j, k), xc_buf.at[j, y, lax.rem(xcore + k, 8)], rr.at[j, xcore], dev_xc(k))
        rr[j, xcore] = xc_buf[j, y, xcore]

    def f_down(j):
        sent(lambda key: key[0] in ("hy", "hx", "core") and key[1] == j)
        down(j, 1, xh.at[j, 0], (4, 4, 2, 16))
        down(j, 2, xh.at[j, 1], (4, 4, 2, 16))
        send(("hcore", j), xh.at[j, 1 - c], hc.at[j], dev_sib)

    def f_x1(j):
        got(("hcore", j))
        for i in range(4):
            tiles(xh.at[j, c, i], xh.at[j, c, i], hc.at[j, i])
        r4_first("rx", j, hotx_at(j), rx_at(j), x, dev_x)

    def f_x2(j):
        r4_second("rx", j, hotx_at(j), rx_at(j), x, dev_x)

    def f_y1(j):
        r4_done("rx", j, hotx_at(j), rx_at(j), x)
        r4_first("rh", j, hoty_at(j), rh_at(j), y, dev_y)

    def f_y2(j):
        r4_second("rh", j, hoty_at(j), rh_at(j), y, dev_y)

    def f_done(j):
        r4_done("rh", j, hoty_at(j), rh_at(j), y)

    def zsend(j, s):
        plus, minus = hops(j)
        if s <= plus:
            send(("rz", j, "p", s), tk.at[j, add(z, plus - s + 1, NZ)], zr.at[j, s - 1], dev_z(1))
        if s <= minus:
            send(("rz", j, "m", s), tk.at[j, add(z, -(minus - s + 1), NZ)], zr.at[j, plus + s - 1], dev_z(-1))

    def g_combine(j):
        for k in range(1, 8):
            got(("back", j, k))

        @pl.loop(0, NT)
        def _(n):
            cols = pl.ds(pl.multiple_of(n * 256, 256), 256)
            cold = rr[j, :, :, cols].reshape(128, 256)
            hot = xh[j, c, x, y, :, :, cols].reshape(32, 256)
            total = jnp.dot(mcomb[0], cold, preferred_element_type=F32)
            total += jnp.dot(mcomb[1], cold, preferred_element_type=F32)
            total += jnp.dot(mcomb[2][:, 0:32], hot, preferred_element_type=F32)
            total += jnp.dot(mcomb[3][:, 0:32], hot, preferred_element_type=F32)
            tk[j, :, :, cols] = total.astype(BF).reshape(8, 16, 256)

        zsend(j, 1)

    def g_step(s, j):
        plus, minus = hops(j)
        if s - 1 <= plus:
            got(("rz", j, "p", s - 1))
            if s <= plus:
                b = add(z, plus - s + 1, NZ)
                summed(tk.at[j, b], tk.at[j, b], zr.at[j, s - 2])
        if s - 1 <= minus:
            got(("rz", j, "m", s - 1))
            if s <= minus:
                b = add(z, -(minus - s + 1), NZ)
                summed(tk.at[j, b], tk.at[j, b], zr.at[j, plus + s - 2])
        if s <= 4:
            zsend(j, s)
        else:
            summed(out_ref.at[:, pl.ds(j * W, W)], tk.at[j, z], zr.at[j, plus - 1], zr.at[j, 6])

    dispatch = [d_zstart] + [functools.partial(d_zstep, s) for s in (2, 3, 4)] + [
        d_select, d_hoty2, d_coldy1, d_hotx1, d_coldy2, d_hotx2, d_coldmm, d_core, d_hotmm]
    order = sorted((s + 2 * j, s, j) for s in range(len(dispatch)) for j in range(CHUNKS))
    done_cold = 0
    queue = []
    for _, s, j in order:
        dispatch[s](j)
        if dispatch[s] is d_coldmm:
            done_cold += 1
            if done_cold == CHUNKS:
                silu_cold()
                for i in range(CHUNKS):
                    e_down(i)
    silu_hot()
    hot = [f_down, f_x1, f_x2, f_y1, f_y2, f_done]
    cold = [None, e_second, e_return]
    last = [g_combine] + [functools.partial(g_step, s) for s in (2, 3, 4, 5)]
    stages = [(f_down,), (e_second, f_x1), (f_x2, e_return), (f_y1,), (f_y2,), (f_done, last[0])] + [(g,) for g in last[1:]]
    order = sorted((s + 2 * j, s, j) for s in range(len(stages)) for j in range(CHUNKS))
    for _, s, j in order:
        for f in stages[s]:
            f(j)
    sent(lambda key: True)


def local(hidden_states, expert_ids, route_weights, w_gate, w_up, w_down):
    rows, width = hidden_states.shape
    topk = expert_ids.shape[1]
    W = width // CHUNKS
    e = lax.axis_index("exp")
    z = e // 8
    flat = expert_ids.reshape(-1)
    token = jnp.arange(rows * topk, dtype=jnp.int32) // topk
    earlier = (flat[:, None] == flat[None, :]) & (token[None, :] < token[:, None])
    rank = jnp.sum(earlier.astype(jnp.int32), axis=1).reshape(rows, topk)
    hot_id = jnp.max(jnp.where(rank >= 2, expert_ids, -1))
    code = (z * 512 + expert_ids * 8 + rank + 1).astype(F32)
    norm = route_weights / jnp.sum(route_weights, axis=1, keepdims=True)
    both = jnp.concatenate([code.T, norm.T], axis=0)
    mine = jnp.arange(128, dtype=jnp.int32) // rows == z
    meta = jnp.where(mine[None, :], jnp.tile(both, (1, NZ)), 0.0)
    hot = jnp.full((8, 128), jnp.where(hot_id == e, 1.0, 0.0), F32)

    vmem = pl.BlockSpec(memory_space=pltpu.VMEM)
    hbm = pl.BlockSpec(memory_space=pl.ANY)
    C = CHUNKS
    scratch = [
        pltpu.VMEM((C, 8, 16, W), BF),
        pltpu.VMEM((8, 16, 128), F32),
        pltpu.VMEM((C, 10, 16, W), BF),
        pltpu.VMEM((C, 4, 8, 16, W), BF),
        pltpu.VMEM((C, 2, 4, 4, 2, 16, W), BF),
        pltpu.VMEM((width, 768), BF),
        pltpu.VMEM((384, width), BF),
        pltpu.VMEM((3, 512, 768), F32),
        pltpu.VMEM((3, 512, 384), BF),
        pltpu.VMEM((C, 6, 4, 16, W), BF),
        pltpu.VMEM((C, 4, 4, 2, 16, W), BF),
        pltpu.VMEM((C, 6, 2, 2, 16, W), BF),
        pltpu.VMEM((C, 6, 16, W), BF),
        pltpu.VMEM((C, 8, 16, W), BF),
        pltpu.VMEM((C, 8, 16, W), BF),
        pltpu.VMEM((C, 7, 16, W), BF),
        pltpu.VMEM((160, 128), BF),
        pltpu.VMEM((4, 128, 128), BF),
        pltpu.SemaphoreType.DMA((C * NSEM + 8,)),
        pltpu.SemaphoreType.DMA((C * NSEM + 8,)),
        pltpu.SemaphoreType.DMA((3,)),
    ]
    return pl.pallas_call(
        kernel,
        out_shape=jax.ShapeDtypeStruct((rows, width), BF),
        in_specs=[vmem, vmem, vmem, hbm, hbm, hbm],
        out_specs=vmem,
        scratch_shapes=scratch,
        compiler_params=pltpu.CompilerParams(
            collective_id=0, has_side_effects=True, vmem_limit_bytes=60 * 1024 * 1024),
    )(hidden_states, meta, hot, w_gate, w_up, w_down)


def solution(mesh):
    in_specs = (
        P(("rep", "exp"), None),
        P(("rep", "exp"), None),
        P(("rep", "exp"), None),
        P("exp", None, "rep"),
        P("exp", None, "rep"),
        P("exp", "rep", None),
    )
    out_specs = P(("rep", "exp"), None)
    return jax.shard_map(local, mesh=mesh, in_specs=in_specs, out_specs=out_specs, check_vma=False)
```

```python
import functools

import jax
import jax.numpy as jnp
from jax import lax
from jax.experimental import pallas as pl
from jax.experimental.pallas import tpu as pltpu
from jax.sharding import PartitionSpec as P

MESH = pl.DeviceIdType.MESH
BF = jnp.bfloat16
F32 = jnp.float32

NZ, NX, NY, NC = 8, 4, 4, 2
CHUNKS = 4
NSEM = 80
ZLAST = (2, 3)

ORDER = (
    ("z1", 2), ("z1", 3), ("z1", 0), ("z1", 1), ("z2", 2), ("z2", 3), ("z2", 0), ("z3", 2), ("z3", 3),
    ("z3", 0), ("z2", 1), ("z4", 2), ("z4", 3), ("z4", 0), ("sel", 3), ("sel", 0), ("hy2", 3), ("z3", 1),
    ("sel", 2), ("hy2", 2), ("z4", 1), ("cy1", 3), ("hx1", 2), ("hy2", 0), ("hx1", 3), ("hx2", 2),
    ("sel", 1), ("cy2", 3), ("hz1", 2), ("hx2", 3), ("hx1", 0), ("hy2", 1), ("hz1", 3), ("cy1", 0),
    ("cy1", 2), ("hz2", 2), ("cy1", 1), ("hx1", 1), ("hz2", 3), ("hx2", 0), ("cmm", 3), ("hz3", 2),
    ("hz3", 3), ("hx2", 1), ("core", 0), ("cy2", 2), ("hz4", 2), ("hz4", 3), ("cy2", 0), ("core", 1),
    ("hmm", 0), ("cy2", 1), ("core", 3), ("hmm", 1), ("core", 2), ("cmm", 2), ("hmm", 3), ("cmm", 0),
    ("cmm", 1), ("silc", 0), ("edn", 1), ("edn", 3), ("edn", 0), ("edn", 2), ("hmm", 2), ("silh", 0),
    ("fdn", 2), ("fdn", 3), ("fdn", 0), ("fz1", 2), ("fz1", 3), ("fx1", 0), ("fdn", 1), ("fz2", 2),
    ("fx2", 0), ("fz2", 3), ("fx1", 1), ("fz3", 2), ("e2", 2), ("fz3", 3), ("e2", 0), ("fx2", 1), ("fz4", 2),
    ("fy1", 0), ("e2", 1), ("e2", 3), ("fz4", 3), ("ret", 0), ("fy1", 1), ("fx1", 2), ("fx1", 3), ("ret", 1),
    ("fy2", 0), ("fx2", 2), ("fx2", 3), ("ret", 2), ("ret", 3), ("fy2", 1), ("fdone", 0), ("comb", 0),
    ("fy1", 2), ("fy1", 3), ("fdone", 1), ("comb", 1), ("fy2", 3), ("fy2", 2), ("fdone", 2), ("comb", 2),
    ("gz2", 1), ("gz2", 0), ("fdone", 3), ("comb", 3), ("gz2", 2), ("gz3", 0), ("gz2", 3), ("gz3", 1),
    ("gz3", 2), ("gz3", 3), ("gz4", 1), ("gz4", 0), ("gz4", 2), ("gz4", 3), ("out", 1), ("out", 2),
    ("out", 0), ("out", 3),
)


def kernel(tok_ref, ids_ref, route_ref, wg_hbm, wu_hbm, wd_hbm, out_ref,
           zt, mt, xs, xc_buf, xh, wgu, wd, acc, act, ry, hc, rx, rh, rr, tk, zr,
           zh, hot_ref, sel, mcomb, send_sem, recv_sem, load_sem):
    y = lax.axis_index("rep")
    e = lax.axis_index("exp")
    z = e // 8
    xcore = lax.rem(e, 8)
    x = xcore // 2
    c = lax.rem(e, 2)
    width = tok_ref.shape[1]
    W = width // CHUNKS
    NT = W // 256
    S = W // NZ
    zcols = pl.ds(pl.multiple_of(z * S, S), S)

    def add(v, k, n):
        return lax.rem(v + (k + n), n)

    def dev_z(k):
        return {"rep": y, "exp": add(z, k, NZ) * 8 + xcore}

    def dev_x(k):
        return {"rep": y, "exp": z * 8 + add(x, k, NX) * 2 + c}

    def dev_y(k):
        return {"rep": add(y, k, NY), "exp": e}

    def dev_xc(k):
        return {"rep": y, "exp": z * 8 + lax.rem(xcore + k, 8)}

    dev_sib = {"rep": y, "exp": z * 8 + x * 2 + (1 - c)}

    loads = [
        pltpu.make_async_copy(wg_hbm.at[0], wgu.at[:, pl.ds(0, 384)], load_sem.at[0]),
        pltpu.make_async_copy(wu_hbm.at[0], wgu.at[:, pl.ds(384, 384)], load_sem.at[1]),
        pltpu.make_async_copy(wd_hbm.at[0], wd, load_sem.at[2]),
    ]
    for cp in loads:
        cp.start()

    barrier = pltpu.get_barrier_semaphore()
    partners = [dev_z(k) for k in range(1, 8)] + [dev_y(1), dev_y(-1)] + [dev_xc(k) for k in range(1, 8)]
    for p in partners:
        pl.semaphore_signal(barrier, inc=1, device_id=p, device_id_type=MESH)

    for j in range(CHUNKS):
        zt[j, z] = tok_ref[:, pl.ds(j * W, W)]

    ids = ids_ref[...]
    route = route_ref[...]
    norm = route / jnp.sum(route, axis=0, keepdims=True)
    expert = lax.broadcasted_iota(jnp.int32, (64, 16), 0)
    named = jnp.zeros((64, 16), F32)
    for k in range(8):
        named = named + jnp.where(ids[k:k + 1, :] == expert, 1.0, 0.0)
    before = (lax.broadcasted_iota(jnp.int32, (16, 16), 0) < lax.broadcasted_iota(jnp.int32, (16, 16), 1))
    earlier = jnp.dot(named.astype(BF), jnp.where(before, 1.0, 0.0).astype(BF), preferred_element_type=F32)
    ranks = [jnp.sum(jnp.where(ids[k:k + 1, :] == expert, earlier, 0.0), axis=0, keepdims=True)
             for k in range(8)]
    rank = jnp.concatenate(ranks, axis=0)
    is_hot = jnp.where((ids == e) & (rank > 1.5), 1.0, 0.0)
    hot_ref[...] = jnp.broadcast_to(jnp.max(jnp.max(is_hot, axis=1, keepdims=True), axis=0, keepdims=True), (8, 128))
    high = norm.astype(BF)
    table = jnp.concatenate([ids.astype(F32), rank, high.astype(F32), norm - high.astype(F32)], axis=0)
    lane = lax.broadcasted_iota(jnp.int32, (16, 128), 1)
    place = jnp.where(lane == z * 16 + lax.broadcasted_iota(jnp.int32, (16, 128), 0), 1.0, 0.0)
    placed = jnp.dot(table.astype(BF), place.astype(BF), preferred_element_type=F32)
    own = (lax.broadcasted_iota(jnp.int32, (8, 128), 1) >> 4) == z
    base = (z * 512 + 1).astype(F32)
    mt[z, 0:8, :] = jnp.where(own, placed[0:8] * 8.0 + placed[8:16] + base, 0.0)
    mt[z, 8:16, :] = placed[16:24] + placed[24:32]

    pl.semaphore_wait(barrier, len(partners))

    count = [0]
    pending = []
    copies = {}

    def send(key, src, dst, dev):
        i = count[0]
        count[0] += 1
        cp = pltpu.make_async_remote_copy(
            src_ref=src, dst_ref=dst, send_sem=send_sem.at[i], recv_sem=recv_sem.at[i],
            device_id=dev, device_id_type=MESH)
        cp.start()
        copies[key] = cp
        pending.append(key)

    def got(key):
        copies[key].wait_recv()

    def sent(match):
        for key in list(pending):
            if match(key):
                copies[key].wait_send()
                pending.remove(key)

    def hops(j):
        return (4, 3) if j % 2 == 0 else (3, 4)

    def zg_start(tag, at, j, s):
        plus, minus = hops(j)
        if s <= plus:
            slot = add(z, -(s - 1), NZ)
            send((tag, j, "p", s), at(slot), at(slot), dev_z(1))
        if s <= minus:
            slot = add(z, s - 1, NZ)
            send((tag, j, "m", s), at(slot), at(slot), dev_z(-1))

    def zg_wait(tag, j, s):
        plus, minus = hops(j)
        if s <= plus:
            got((tag, j, "p", s))
        if s <= minus:
            got((tag, j, "m", s))

    def g4_first(tag, j, at, me, dev):
        send((tag, j, "p1"), at(me, None), at(me, None), dev(1))
        send((tag, j, "m1"), at(me, None), at(me, None), dev(-1))

    def g4_second(tag, j, at, me, dev):
        left, right = add(me, -1, 4), add(me, 1, 4)
        got((tag, j, "p1"))
        send((tag, j, "p2"), at(left, 0), at(left, 0), dev(1))
        got((tag, j, "m1"))
        send((tag, j, "m2"), at(right, 1), at(right, 1), dev(-1))

    def g4_done(tag, j):
        got((tag, j, "p2"))
        got((tag, j, "m2"))

    def r4_first(tag, j, at, slot, me, dev):
        left, right, far = add(me, -1, 4), add(me, 1, 4), add(me, 2, 4)
        send((tag, j, 0), at(far, 0), slot(0), dev(1))
        send((tag, j, 2), at(far, 1), slot(2), dev(-1))
        send((tag, j, 1), at(right, 1), slot(1), dev(1))
        send((tag, j, 3), at(left, 0), slot(3), dev(-1))

    def summed(dst, *parts):
        total = parts[0][...].astype(F32)
        for part in parts[1:]:
            total = total + part[...].astype(F32)
        dst[...] = total.astype(BF)

    def tiles(dst, *parts):
        if dst.shape[-1] < 256:
            summed(dst, *parts)
            return

        @pl.loop(0, NT)
        def _(n):
            cols = pl.ds(pl.multiple_of(n * 256, 256), 256)
            lead = (slice(None),) * (len(dst.shape) - 1)
            summed(dst.at[lead + (cols,)], *[p.at[lead + (cols,)] for p in parts])

    def r4_second(tag, j, at, slot, me, dev):
        left, right = add(me, -1, 4), add(me, 1, 4)
        got((tag, j, 0))
        tiles(at(right, 0), at(right, 0), slot(0))
        send((tag, j, 4), at(right, 0), slot(4), dev(1))
        got((tag, j, 2))
        tiles(at(left, 1), at(left, 1), slot(2))
        send((tag, j, 5), at(left, 1), slot(5), dev(-1))

    def r4_done(tag, j, at, slot, me):
        for k in (1, 3, 4, 5):
            got((tag, j, k))
        tiles(at(me, 0), at(me, 0), slot(3), slot(4))
        tiles(at(me, 1), at(me, 1), slot(1), slot(5))

    def cold_at(j):
        def at(i, half):
            return xc_buf.at[j, i] if half is None else xc_buf.at[j, i, pl.ds(4 * half, 4)]
        return at

    def hoty_at(j):
        def at(i, half):
            if j in ZLAST:
                return xh.at[j, c, x, i, :, :, zcols] if half is None else xh.at[j, c, x, i, half, :, zcols]
            return xh.at[j, c, x, i] if half is None else xh.at[j, c, x, i, half]
        return at

    def hotx_at(j):
        def at(i, half):
            if j in ZLAST:
                if half is None:
                    return xh.at[j, c, i, :, :, :, zcols]
                return xh.at[j, c, i, pl.ds(2 * half, 2), :, :, zcols]
            return xh.at[j, c, i] if half is None else xh.at[j, c, i, pl.ds(2 * half, 2)]
        return at

    def slice_at(j):
        return lambda k: xh.at[j, c, :, :, :, :, pl.ds(pl.multiple_of(k * S, S), S)]

    def meta_done():
        both = mt[0]
        for k in range(1, NZ):
            both = both + mt[k]
        codes = both[0:8].astype(jnp.int32) - 1
        weights = both[8:16]
        row = lax.broadcasted_iota(jnp.int32, (128, 128), 0)
        want = ((row >> 1) & 7) * 512 + (z * 8 + (row >> 4)) * 8 + (row & 1)
        pick = jnp.zeros((128, 128), F32)
        comb = jnp.zeros((128, 128), F32)
        for k in range(8):
            hit = codes[k:k + 1, :] == want
            pick = pick + jnp.where(hit, 1.0, 0.0)
            comb = comb + jnp.where(hit, weights[k:k + 1, :], 0.0)
        sel[0:128, :] = pick.astype(BF)
        comb = comb.T
        high = comb.astype(BF)
        mcomb[0] = high
        mcomb[1] = (comb - high.astype(F32)).astype(BF)
        want = (row >> 2) * 512 + (row & 3) + 2
        masked = (codes >> 9) * 512 + (codes & 7)
        pick = jnp.zeros((128, 128), F32)
        comb = jnp.zeros((128, 128), F32)
        for k in range(8):
            hit = masked[k:k + 1, :] == want
            pick = pick + jnp.where(hit, 1.0, 0.0)
            comb = comb + jnp.where(hit, weights[k:k + 1, :], 0.0)
        sel[128:160, :] = pick[0:32, :].astype(BF)
        comb = comb.T
        high = comb.astype(BF)
        mcomb[2] = high
        mcomb[3] = (comb - high.astype(F32)).astype(BF)

    def d_zstart(j):
        zg_start("z", lambda s: zt.at[j, s], j, 1)
        if j == 0:
            for k in range(1, NZ):
                send(("meta", k), mt.at[z], mt.at[z], dev_z(k))

    def d_zstep(s, j):
        zg_wait("z", j, s - 1)
        zg_start("z", lambda i: zt.at[j, i], j, s)

    ready = []
    started = set()

    def d_select(j):
        if not ready:
            ready.append(j)
            for k in range(1, NZ):
                got(("meta", k))
            meta_done()
        zg_wait("z", j, 4)

        @pl.loop(0, NT)
        def _(n):
            cols = pl.ds(pl.multiple_of(n * 256, 256), 256)
            rows = jnp.dot(sel[...], zt[j, :, :, cols].reshape(128, 256), preferred_element_type=F32)
            xs[j, :, :, cols] = rows.astype(BF).reshape(10, 16, 256)

        for k in range(1, 8):
            send(("x", j, k), xs.at[j, lax.rem(xcore + k, 8)], xc_buf.at[j, y, xcore], dev_xc(k))
        if j in ZLAST:
            xh[j, c, x, y, :, :, zcols] = xs[j, 8:10, :, zcols]
        else:
            xh[j, c, x, y] = xs[j, 8:10]
        g4_first("hy", j, hoty_at(j), y, dev_y)
        xc_buf[j, y, xcore] = xs[j, xcore]

    def d_hoty2(j):
        g4_second("hy", j, hoty_at(j), y, dev_y)

    def d_coldy1(j):
        for k in range(1, 8):
            got(("x", j, k))
        g4_first("cy", j, cold_at(j), y, dev_y)

    def d_hotx1(j):
        g4_done("hy", j)
        g4_first("hx", j, hotx_at(j), x, dev_x)

    def d_coldy2(j):
        g4_second("cy", j, cold_at(j), y, dev_y)

    def d_hotx2(j):
        g4_second("hx", j, hotx_at(j), x, dev_x)

    def d_hotz(s, j):
        if s == 1:
            g4_done("hx", j)
        else:
            zg_wait("hz", j, s - 1)
        zg_start("hz", slice_at(j), j, s)

    def gate_up(j, block, at):
        first = block not in started
        started.add(block)

        @pl.loop(0, 3)
        def _(n):
            cols = pl.ds(pl.multiple_of(n * 256, 256), 256)
            part = jnp.dot(at[...].reshape(512, W), wgu[pl.ds(j * W, W), cols],
                           preferred_element_type=F32)
            if first:
                acc[block, :, cols] = part
            else:
                acc[block, :, cols] += part

    def weights_in():
        if not started:
            loads[0].wait()
            loads[1].wait()

    def d_coldmm(j):
        g4_done("cy", j)
        weights_in()
        gate_up(j, 0, xc_buf.at[j])

    def d_core(j):
        if j in ZLAST:
            zg_wait("hz", j, 4)
        else:
            g4_done("hx", j)
        send(("core", j), xh.at[j, c], xh.at[j, c], dev_sib)

    def d_hotmm(j):
        got(("core", j))
        weights_in()
        gate_up(j, 1, xh.at[j, 0])
        gate_up(j, 2, xh.at[j, 1])

    def activate(block, masked):
        @pl.loop(0, 8)
        def _(i):
            rows = pl.ds(pl.multiple_of(i * 64, 64), 64)
            gate = acc[block, rows, 0:384]
            up = acc[block, rows, 384:768]
            value = gate / (1.0 + jnp.exp(-gate)) * up
            if masked:
                value = jnp.where(hot_ref[0:1, 0:1] > 0.5, value, 0.0)
            act[block, rows, :] = value.astype(BF)

    def down(j, block, at, shape):
        @pl.loop(0, NT)
        def _(n):
            cols = pl.ds(pl.multiple_of(n * 256, 256), 256)
            wcols = pl.ds(pl.multiple_of(j * W + n * 256, 256), 256)
            part = jnp.dot(act[block], wd[:, wcols], preferred_element_type=F32)
            at[(slice(None),) * len(shape) + (cols,)] = part.astype(BF).reshape(shape + (256,))

    def silu_cold(j):
        loads[2].wait()
        activate(0, False)

    def silu_hot(j):
        activate(1, True)
        activate(2, True)

    def ry_at(j):
        return lambda k: ry.at[j, k]

    def rx_at(j):
        if j in ZLAST:
            return lambda k: rx.at[j, k, :, :, :, pl.ds(0, S)]
        return lambda k: rx.at[j, k]

    def rh_at(j):
        if j in ZLAST:
            return lambda k: rh.at[j, k, :, pl.ds(0, S)]
        return lambda k: rh.at[j, k]

    def e_down(j):
        sent(lambda key: key[0] == "cy" and key[1] == j)
        down(j, 0, xc_buf.at[j], (4, 8, 16))
        r4_first("ry", j, cold_at(j), ry_at(j), y, dev_y)

    def e_second(j):
        r4_second("ry", j, cold_at(j), ry_at(j), y, dev_y)

    def e_return(j):
        r4_done("ry", j, cold_at(j), ry_at(j), y)
        for k in range(1, 8):
            send(("back", j, k), xc_buf.at[j, y, lax.rem(xcore + k, 8)], rr.at[j, xcore], dev_xc(k))
        rr[j, xcore] = xc_buf[j, y, xcore]

    def f_down(j):
        sent(lambda key: key[0] in ("hy", "hx", "hz", "core") and key[1] == j)
        down(j, 1, xh.at[j, 0], (4, 4, 2, 16))
        down(j, 2, xh.at[j, 1], (4, 4, 2, 16))
        send(("hcore", j), xh.at[j, 1 - c], hc.at[j], dev_sib)

    def core_sum(j):
        got(("hcore", j))
        for i in range(4):
            tiles(xh.at[j, c, i], xh.at[j, c, i], hc.at[j, i])

    def ring_send(tag, j, s, block, slot):
        plus, minus = hops(j)
        if s <= plus:
            send((tag, j, "p", s), block(add(z, plus - s + 1, NZ)), slot(s - 1), dev_z(1))
        if s <= minus:
            send((tag, j, "m", s), block(add(z, -(minus - s + 1), NZ)), slot(plus + s - 1), dev_z(-1))

    def ring_sum(tag, j, s, block, slot):
        plus, minus = hops(j)
        if s - 1 <= plus:
            got((tag, j, "p", s - 1))
            if s <= plus:
                b = add(z, plus - s + 1, NZ)
                summed(block(b), block(b), slot(s - 2))
        if s - 1 <= minus:
            got((tag, j, "m", s - 1))
            if s <= minus:
                b = add(z, -(minus - s + 1), NZ)
                summed(block(b), block(b), slot(plus + s - 2))

    def zh_at(j):
        return lambda k: zh.at[ZLAST.index(j), k]

    def f_z(s, j):
        if s == 1:
            core_sum(j)
        else:
            ring_sum("fz", j, s, slice_at(j), zh_at(j))
        ring_send("fz", j, s, slice_at(j), zh_at(j))

    def f_x1(j):
        if j in ZLAST:
            ring_sum("fz", j, 5, slice_at(j), zh_at(j))
            mine = slice_at(j)(z)
            summed(mine, mine, zh_at(j)(hops(j)[0] - 1), zh_at(j)(6))
        else:
            core_sum(j)
        r4_first("rx", j, hotx_at(j), rx_at(j), x, dev_x)

    def f_x2(j):
        r4_second("rx", j, hotx_at(j), rx_at(j), x, dev_x)

    def f_y1(j):
        r4_done("rx", j, hotx_at(j), rx_at(j), x)
        r4_first("rh", j, hoty_at(j), rh_at(j), y, dev_y)

    def f_y2(j):
        r4_second("rh", j, hoty_at(j), rh_at(j), y, dev_y)

    def f_done(j):
        r4_done("rh", j, hoty_at(j), rh_at(j), y)

    def tk_at(j):
        return lambda k: tk.at[j, k]

    def zr_at(j):
        return lambda k: zr.at[j, k]

    def g_combine(j):
        for k in range(1, 8):
            got(("back", j, k))

        @pl.loop(0, NT)
        def _(n):
            cols = pl.ds(pl.multiple_of(n * 256, 256), 256)
            cold = rr[j, :, :, cols].reshape(128, 256)
            total = jnp.dot(mcomb[0], cold, preferred_element_type=F32)
            total += jnp.dot(mcomb[1], cold, preferred_element_type=F32)
            if j not in ZLAST:
                total += hot_part(xh[j, c, x, y, :, :, cols].reshape(32, 256))
            tk[j, :, :, cols] = total.astype(BF).reshape(8, 16, 256)

        if j in ZLAST:
            cold = rr[j, :, :, zcols].reshape(128, S)
            total = jnp.dot(mcomb[0], cold, preferred_element_type=F32)
            total += jnp.dot(mcomb[1], cold, preferred_element_type=F32)
            total += hot_part(xh[j, c, x, y, :, :, zcols].reshape(32, S))
            tk[j, :, :, zcols] = total.astype(BF).reshape(8, 16, S)
        ring_send("rz", j, 1, tk_at(j), zr_at(j))

    def hot_part(rows):
        total = jnp.dot(mcomb[2][:, 0:32], rows, preferred_element_type=F32)
        return total + jnp.dot(mcomb[3][:, 0:32], rows, preferred_element_type=F32)

    def g_step(s, j):
        ring_sum("rz", j, s, tk_at(j), zr_at(j))
        ring_send("rz", j, s, tk_at(j), zr_at(j))

    def g_out(j):
        ring_sum("rz", j, 5, tk_at(j), zr_at(j))
        summed(out_ref.at[:, pl.ds(j * W, W)], tk.at[j, z], zr.at[j, hops(j)[0] - 1], zr.at[j, 6])

    def stepped(f):
        return [functools.partial(f, s) for s in range(1, 5)]

    steps = {
        "z1": d_zstart, "sel": d_select, "hy2": d_hoty2, "hx1": d_hotx1, "hx2": d_hotx2, "core": d_core,
        "cy1": d_coldy1, "cy2": d_coldy2, "cmm": d_coldmm, "hmm": d_hotmm, "silc": silu_cold,
        "silh": silu_hot, "edn": e_down, "e2": e_second, "ret": e_return, "fdn": f_down, "fx1": f_x1,
        "fx2": f_x2, "fy1": f_y1, "fy2": f_y2, "fdone": f_done, "comb": g_combine, "out": g_out,
    }
    for name, f in (("z", d_zstep), ("hz", d_hotz), ("fz", f_z), ("gz", g_step)):
        for s, g in enumerate(stepped(f), 1):
            steps.setdefault(name + str(s), g)
    for name, j in ORDER:
        steps[name](j)
    sent(lambda key: True)


def local(hidden_states, expert_ids, route_weights, w_gate, w_up, w_down):
    rows, width = hidden_states.shape
    W = width // CHUNKS
    vmem = pl.BlockSpec(memory_space=pltpu.VMEM)
    hbm = pl.BlockSpec(memory_space=pl.ANY)
    C = CHUNKS
    scratch = [
        pltpu.VMEM((C, 8, 16, W), BF),
        pltpu.VMEM((8, 16, 128), F32),
        pltpu.VMEM((C, 10, 16, W), BF),
        pltpu.VMEM((C, 4, 8, 16, W), BF),
        pltpu.VMEM((C, 2, 4, 4, 2, 16, W), BF),
        pltpu.VMEM((width, 768), BF),
        pltpu.VMEM((384, width), BF),
        pltpu.VMEM((3, 512, 768), F32),
        pltpu.VMEM((3, 512, 384), BF),
        pltpu.VMEM((C, 6, 4, 16, W), BF),
        pltpu.VMEM((C, 4, 4, 2, 16, W), BF),
        pltpu.VMEM((C, 6, 2, 2, 16, W), BF),
        pltpu.VMEM((C, 6, 16, W), BF),
        pltpu.VMEM((C, 8, 16, W), BF),
        pltpu.VMEM((C, 8, 16, W), BF),
        pltpu.VMEM((C, 7, 16, W), BF),
        pltpu.VMEM((len(ZLAST), 7, 4, 4, 2, 16, W // NZ), BF),
        pltpu.VMEM((8, 128), F32),
        pltpu.VMEM((160, 128), BF),
        pltpu.VMEM((4, 128, 128), BF),
        pltpu.SemaphoreType.DMA((C * NSEM + 8,)),
        pltpu.SemaphoreType.DMA((C * NSEM + 8,)),
        pltpu.SemaphoreType.DMA((3,)),
    ]
    return pl.pallas_call(
        kernel,
        out_shape=jax.ShapeDtypeStruct((rows, width), BF),
        in_specs=[vmem, vmem, vmem, hbm, hbm, hbm],
        out_specs=vmem,
        scratch_shapes=scratch,
        compiler_params=pltpu.CompilerParams(
            collective_id=0, has_side_effects=True, vmem_limit_bytes=60 * 1024 * 1024),
    )(hidden_states, expert_ids.T, route_weights.T, w_gate, w_up, w_down)


def solution(mesh):
    in_specs = (
        P(("rep", "exp"), None),
        P(("rep", "exp"), None),
        P(("rep", "exp"), None),
        P("exp", None, "rep"),
        P("exp", None, "rep"),
        P("exp", "rep", None),
    )
    out_specs = P(("rep", "exp"), None)
    return jax.shard_map(local, mesh=mesh, in_specs=in_specs, out_specs=out_specs, check_vma=False)
```

```python
import functools

import jax
import jax.numpy as jnp
from jax import lax
from jax.experimental import pallas as pl
from jax.experimental.pallas import tpu as pltpu
from jax.sharding import PartitionSpec as P

MESH = pl.DeviceIdType.MESH
BF = jnp.bfloat16
F32 = jnp.float32

NZ, NX, NY, NC = 8, 4, 4, 2
WIDTHS = (1024, 1024, 512, 512, 512, 512)
ZLAST = (0, 1)
ZDIR = ()
RDIR = (0, 1)
CHUNKS = len(WIDTHS)
OFFS = tuple(sum(WIDTHS[:i]) for i in range(CHUNKS))
NSEM = 80

ORDER = (
    ("z1", 2), ("z1", 3), ("z1", 1), ("z1", 4), ("z1", 0), ("z2", 2), ("z1", 5), ("z2", 3), ("z2", 1),
    ("z2", 4), ("z2", 0), ("z3", 2), ("z2", 5), ("z3", 3), ("z3", 1), ("z3", 4), ("z3", 0), ("z4", 2),
    ("z4", 3), ("z4", 1), ("z3", 5), ("z4", 4), ("z4", 0), ("selh", 2), ("selc", 2), ("selh", 3),
    ("selc", 3), ("selh", 1), ("selc", 1), ("hy2", 2), ("selh", 4), ("selh", 0), ("hy2", 3), ("cy1", 2),
    ("z4", 5), ("hx1", 1), ("selc", 4), ("cy1", 3), ("hx1", 0), ("hx1", 2), ("selh", 5), ("hy2", 4),
    ("hz1", 1), ("cy1", 1), ("selc", 0), ("hz1", 0), ("cy1", 4), ("hx1", 4), ("hz2", 1), ("hy2", 5),
    ("selc", 5), ("cy2", 2), ("hx2", 2), ("hz2", 0), ("cy2", 3), ("cy2", 1), ("hx2", 4), ("hz3", 1),
    ("hx1", 3), ("cy1", 0), ("hz3", 0), ("hx1", 5), ("cy1", 5), ("core", 4), ("core", 2), ("hz4", 1),
    ("cmm", 3), ("hx2", 3), ("hmm", 4), ("cmm", 1), ("hz4", 0), ("hmm", 2), ("hx2", 5), ("core", 3),
    ("cy2", 4), ("core", 1), ("cmm", 2), ("hmm", 3), ("cy2", 0), ("core", 5), ("core", 0), ("hmm", 1),
    ("cy2", 5), ("hmm", 5), ("cmm", 4), ("hmm", 0), ("silh", 0), ("cmm", 0), ("cmm", 5), ("silc", 0),
    ("edn", 3), ("fdn", 4), ("fdn", 1), ("edn", 5), ("fx1", 4), ("fdn", 5), ("edn", 4), ("fz1", 1),
    ("fx1", 5), ("edn", 2), ("fdn", 2), ("e2", 3), ("fx2", 4), ("edn", 1), ("fdn", 0), ("fx2", 5),
    ("fz2", 1), ("fdn", 3), ("fx1", 2), ("fz1", 0), ("fx1", 3), ("fz3", 1), ("fx2", 2), ("e2", 5), ("e2", 2),
    ("fx2", 3), ("e2", 4), ("fz2", 0), ("fy1", 5), ("fy1", 4), ("ret", 3), ("fy1", 2), ("ret", 5),
    ("fz4", 1), ("fy1", 3), ("e2", 1), ("fy2", 5), ("fy2", 4), ("fz3", 0), ("ret", 4), ("fy2", 2),
    ("fy2", 3), ("ret", 2), ("edn", 0), ("fx1", 1), ("ret", 1), ("fdone", 5), ("comb", 5), ("fz4", 0),
    ("fdone", 2), ("fdone", 3), ("fdone", 4), ("comb", 4), ("comb", 3), ("fy1", 1), ("e2", 0), ("comb", 2),
    ("gz2", 5), ("fx1", 0), ("gz2", 4), ("fdone", 1), ("gz2", 3), ("gz2", 2), ("comb", 1), ("ret", 0),
    ("gz3", 4), ("gz3", 3), ("gz3", 2), ("gz3", 5), ("fy1", 0), ("fdone", 0), ("comb", 0), ("out", 1),
    ("gz4", 5), ("gz4", 3), ("gz4", 4), ("gz4", 2), ("out", 4), ("out", 5), ("out", 2), ("out", 3),
    ("out", 0),
)


def kernel(tok_ref, ids_ref, route_ref, wg_hbm, wu_hbm, wd_hbm, out_ref,
           zt, mt, xs, xc_buf, xh, wgu, wd, acc, act, ry, hc, rx, rh, rr, tk, zr,
           zh, hot_ref, sel, mcomb, send_sem, recv_sem, load_sem):
    y = lax.axis_index("rep")
    e = lax.axis_index("exp")
    z = e // 8
    xcore = lax.rem(e, 8)
    x = xcore // 2
    c = lax.rem(e, 2)

    def part_of(j, k):
        S = WIDTHS[j] // NZ
        return pl.ds(pl.multiple_of(k * S, S), S)

    def add(v, k, n):
        return lax.rem(v + (k + n), n)

    def dev_z(k):
        return {"rep": y, "exp": add(z, k, NZ) * 8 + xcore}

    def dev_x(k):
        return {"rep": y, "exp": z * 8 + add(x, k, NX) * 2 + c}

    def dev_y(k):
        return {"rep": add(y, k, NY), "exp": e}

    def dev_xc(k):
        return {"rep": y, "exp": z * 8 + lax.rem(xcore + k, 8)}

    dev_sib = {"rep": y, "exp": z * 8 + x * 2 + (1 - c)}

    loads = [
        pltpu.make_async_copy(wg_hbm.at[0], wgu.at[:, pl.ds(0, 384)], load_sem.at[0]),
        pltpu.make_async_copy(wu_hbm.at[0], wgu.at[:, pl.ds(384, 384)], load_sem.at[1]),
        pltpu.make_async_copy(wd_hbm.at[0], wd, load_sem.at[2]),
    ]
    for cp in loads:
        cp.start()

    barrier = pltpu.get_barrier_semaphore()
    partners = [dev_z(k) for k in range(1, 8)] + [dev_y(k) for k in range(1, 4)] + [dev_xc(k) for k in range(1, 8)]
    for p in partners:
        pl.semaphore_signal(barrier, inc=1, device_id=p, device_id_type=MESH)

    for j in range(CHUNKS):
        zt[j][z] = tok_ref[:, pl.ds(OFFS[j], WIDTHS[j])]

    ids = ids_ref[...]
    route = route_ref[...]
    norm = route / jnp.sum(route, axis=0, keepdims=True)
    expert = lax.broadcasted_iota(jnp.int32, (64, 16), 0)
    named = jnp.zeros((64, 16), F32)
    for k in range(8):
        named = named + jnp.where(ids[k:k + 1, :] == expert, 1.0, 0.0)
    before = (lax.broadcasted_iota(jnp.int32, (16, 16), 0) < lax.broadcasted_iota(jnp.int32, (16, 16), 1))
    earlier = jnp.dot(named.astype(BF), jnp.where(before, 1.0, 0.0).astype(BF), preferred_element_type=F32)
    ranks = [jnp.sum(jnp.where(ids[k:k + 1, :] == expert, earlier, 0.0), axis=0, keepdims=True)
             for k in range(8)]
    rank = jnp.concatenate(ranks, axis=0)
    is_hot = jnp.where((ids == e) & (rank > 1.5), 1.0, 0.0)
    hot_ref[...] = jnp.broadcast_to(jnp.max(jnp.max(is_hot, axis=1, keepdims=True), axis=0, keepdims=True), (8, 128))
    high = norm.astype(BF)
    table = jnp.concatenate([ids.astype(F32), rank, high.astype(F32), norm - high.astype(F32)], axis=0)
    lane = lax.broadcasted_iota(jnp.int32, (16, 128), 1)
    place = jnp.where(lane == z * 16 + lax.broadcasted_iota(jnp.int32, (16, 128), 0), 1.0, 0.0)
    placed = jnp.dot(table.astype(BF), place.astype(BF), preferred_element_type=F32)
    own = (lax.broadcasted_iota(jnp.int32, (8, 128), 1) >> 4) == z
    base = (z * 512 + 1).astype(F32)
    mt[z, 0:8, :] = jnp.where(own, placed[0:8] * 8.0 + placed[8:16] + base, 0.0)
    mt[z, 8:16, :] = placed[16:24] + placed[24:32]

    pl.semaphore_wait(barrier, len(partners))

    count = [0]
    pending = []
    copies = {}

    def send(key, src, dst, dev):
        i = count[0]
        count[0] += 1
        cp = pltpu.make_async_remote_copy(
            src_ref=src, dst_ref=dst, send_sem=send_sem.at[i], recv_sem=recv_sem.at[i],
            device_id=dev, device_id_type=MESH)
        cp.start()
        copies[key] = cp
        pending.append(key)

    def got(key):
        copies[key].wait_recv()

    def sent(match):
        for key in list(pending):
            if match(key):
                copies[key].wait_send()
                pending.remove(key)

    def hops(j):
        return (4, 3) if j % 2 == 0 else (3, 4)

    def zg_start(tag, at, j, s):
        plus, minus = hops(j)
        if s <= plus:
            slot = add(z, -(s - 1), NZ)
            send((tag, j, "p", s), at(slot), at(slot), dev_z(1))
        if s <= minus:
            slot = add(z, s - 1, NZ)
            send((tag, j, "m", s), at(slot), at(slot), dev_z(-1))

    def zg_wait(tag, j, s):
        plus, minus = hops(j)
        if s <= plus:
            got((tag, j, "p", s))
        if s <= minus:
            got((tag, j, "m", s))

    def g4_first(tag, j, at, me, dev):
        send((tag, j, "p1"), at(me, None), at(me, None), dev(1))
        send((tag, j, "m1"), at(me, None), at(me, None), dev(-1))

    def g4_second(tag, j, at, me, dev):
        left, right = add(me, -1, 4), add(me, 1, 4)
        got((tag, j, "p1"))
        send((tag, j, "p2"), at(left, 0), at(left, 0), dev(1))
        got((tag, j, "m1"))
        send((tag, j, "m2"), at(right, 1), at(right, 1), dev(-1))

    def g4_done(tag, j):
        got((tag, j, "p2"))
        got((tag, j, "m2"))

    def d4_send(tag, j, at, me, dev):
        for k in (2, 1, 3):
            send((tag, j, k), at(me, None), at(me, None), dev(k))

    def d4_wait(tag, j):
        for k in (1, 2, 3):
            got((tag, j, k))

    def d4_reduce(tag, j, at, slot, me, dev):
        for k in (2, 1, 3):
            send((tag, j, k), at(add(me, k, 4), None), slot(k - 1), dev(k))

    def d4_sum(tag, j, at, slot, me):
        d4_wait(tag, j)
        tiles(at(me, None), at(me, None), slot(0), slot(1), slot(2))

    def r4_first(tag, j, at, slot, me, dev):
        left, right, far = add(me, -1, 4), add(me, 1, 4), add(me, 2, 4)
        send((tag, j, 0), at(far, 0), slot(0), dev(1))
        send((tag, j, 2), at(far, 1), slot(2), dev(-1))
        send((tag, j, 1), at(right, 1), slot(1), dev(1))
        send((tag, j, 3), at(left, 0), slot(3), dev(-1))

    def summed(dst, *parts):
        total = parts[0][...].astype(F32)
        for part in parts[1:]:
            total = total + part[...].astype(F32)
        dst[...] = total.astype(BF)

    def tiles(dst, *parts):
        if dst.shape[-1] < 256:
            summed(dst, *parts)
            return

        @pl.loop(0, dst.shape[-1] // 256, unroll=True)
        def _(n):
            cols = pl.ds(pl.multiple_of(n * 256, 256), 256)
            lead = (slice(None),) * (len(dst.shape) - 1)
            summed(dst.at[lead + (cols,)], *[p.at[lead + (cols,)] for p in parts])

    def r4_second(tag, j, at, slot, me, dev):
        left, right = add(me, -1, 4), add(me, 1, 4)
        got((tag, j, 0))
        tiles(at(right, 0), at(right, 0), slot(0))
        send((tag, j, 4), at(right, 0), slot(4), dev(1))
        got((tag, j, 2))
        tiles(at(left, 1), at(left, 1), slot(2))
        send((tag, j, 5), at(left, 1), slot(5), dev(-1))

    def r4_done(tag, j, at, slot, me):
        for k in (1, 3, 4, 5):
            got((tag, j, k))
        tiles(at(me, 0), at(me, 0), slot(3), slot(4))
        tiles(at(me, 1), at(me, 1), slot(1), slot(5))

    def cold_at(j):
        def at(i, half):
            return xc_buf[j].at[i] if half is None else xc_buf[j].at[i, pl.ds(4 * half, 4)]
        return at

    def hoty_at(j):
        def at(i, half):
            if j in ZLAST:
                return xh[j].at[c, x, i, :, :, part_of(j, z)] if half is None else xh[j].at[c, x, i, half, :, part_of(j, z)]
            return xh[j].at[c, x, i] if half is None else xh[j].at[c, x, i, half]
        return at

    def hotx_at(j):
        def at(i, half):
            if j in ZLAST:
                if half is None:
                    return xh[j].at[c, i, :, :, :, part_of(j, z)]
                return xh[j].at[c, i, pl.ds(2 * half, 2), :, :, part_of(j, z)]
            return xh[j].at[c, i] if half is None else xh[j].at[c, i, pl.ds(2 * half, 2)]
        return at

    def slice_at(j):
        return lambda k: xh[j].at[c, :, :, :, :, part_of(j, k)]

    def meta_done():
        both = mt[0]
        for k in range(1, NZ):
            both = both + mt[k]
        codes = both[0:8].astype(jnp.int32) - 1
        weights = both[8:16]
        row = lax.broadcasted_iota(jnp.int32, (128, 128), 0)
        want = ((row >> 1) & 7) * 512 + (z * 8 + (row >> 4)) * 8 + (row & 1)
        pick = jnp.zeros((128, 128), F32)
        comb = jnp.zeros((128, 128), F32)
        for k in range(8):
            hit = codes[k:k + 1, :] == want
            pick = pick + jnp.where(hit, 1.0, 0.0)
            comb = comb + jnp.where(hit, weights[k:k + 1, :], 0.0)
        sel[0:128, :] = pick.astype(BF)
        comb = comb.T
        high = comb.astype(BF)
        mcomb[0] = high
        mcomb[1] = (comb - high.astype(F32)).astype(BF)
        want = (row >> 2) * 512 + (row & 3) + 2
        masked = (codes >> 9) * 512 + (codes & 7)
        pick = jnp.zeros((128, 128), F32)
        comb = jnp.zeros((128, 128), F32)
        for k in range(8):
            hit = masked[k:k + 1, :] == want
            pick = pick + jnp.where(hit, 1.0, 0.0)
            comb = comb + jnp.where(hit, weights[k:k + 1, :], 0.0)
        sel[128:160, :] = pick[0:32, :].astype(BF)
        comb = comb.T
        high = comb.astype(BF)
        mcomb[2] = high
        mcomb[3] = (comb - high.astype(F32)).astype(BF)

    def d_zstart(j):
        if not copies:
            for k in range(1, NZ):
                send(("meta", k), mt.at[z], mt.at[z], dev_z(k))
        if j in ZDIR:
            for k in (4, 1, 7, 2, 6, 3, 5):
                send(("z", j, k), zt[j].at[z], zt[j].at[z], dev_z(k))
        else:
            zg_start("z", lambda s: zt[j].at[s], j, 1)

    def d_zstep(s, j):
        zg_wait("z", j, s - 1)
        zg_start("z", lambda i: zt[j].at[i], j, s)

    ready = []
    arrived = []
    started = set()

    def picked(j, first, groups, row):
        if not ready:
            ready.append(j)
            for k in range(1, NZ):
                got(("meta", k))
            meta_done()
        if j not in arrived:
            arrived.append(j)
            if j in ZDIR:
                for k in range(1, NZ):
                    got(("z", j, k))
            else:
                zg_wait("z", j, 4)

        @pl.loop(0, WIDTHS[j] // 256, unroll=True)
        def _(n):
            cols = pl.ds(pl.multiple_of(n * 256, 256), 256)
            rows = jnp.dot(sel[row:row + 16 * groups, :], zt[j][:, :, cols].reshape(128, 256),
                           preferred_element_type=F32)
            xs[j][first:first + groups, :, cols] = rows.astype(BF).reshape(groups, 16, 256)

    def d_pickcold(j):
        picked(j, 0, 8, 0)
        for k in range(1, 8):
            send(("x", j, k), xs[j].at[lax.rem(xcore + k, 8)], xc_buf[j].at[y, xcore], dev_xc(k))
        xc_buf[j][y, xcore] = xs[j][xcore]

    def d_pickhot(j):
        picked(j, 8, 2, 128)
        if j in ZLAST:
            xh[j][c, x, y, :, :, part_of(j, z)] = xs[j][8:10, :, part_of(j, z)]
            d4_send("hy", j, hoty_at(j), y, dev_y)
        else:
            xh[j][c, x, y] = xs[j][8:10]
            g4_first("hy", j, hoty_at(j), y, dev_y)

    def d_hoty2(j):
        g4_second("hy", j, hoty_at(j), y, dev_y)

    def d_coldy1(j):
        for k in range(1, 8):
            got(("x", j, k))
        g4_first("cy", j, cold_at(j), y, dev_y)

    def d_hotx1(j):
        if j in ZLAST:
            d4_wait("hy", j)
            d4_send("hx", j, hotx_at(j), x, dev_x)
        else:
            g4_done("hy", j)
            g4_first("hx", j, hotx_at(j), x, dev_x)

    def d_coldy2(j):
        g4_second("cy", j, cold_at(j), y, dev_y)

    def d_hotx2(j):
        g4_second("hx", j, hotx_at(j), x, dev_x)

    def d_hotz(s, j):
        if s == 1:
            d4_wait("hx", j)
        else:
            zg_wait("hz", j, s - 1)
        zg_start("hz", slice_at(j), j, s)

    def gate_up(j, block, at):
        first = block not in started
        started.add(block)

        @pl.loop(0, 3, unroll=True)
        def _(n):
            cols = pl.ds(pl.multiple_of(n * 256, 256), 256)
            part = jnp.dot(at[...].reshape(512, WIDTHS[j]), wgu[pl.ds(OFFS[j], WIDTHS[j]), cols],
                           preferred_element_type=F32)
            if first:
                acc[block, :, cols] = part
            else:
                acc[block, :, cols] += part

    def weights_in():
        if not started:
            loads[0].wait()
            loads[1].wait()

    def d_coldmm(j):
        g4_done("cy", j)
        weights_in()
        gate_up(j, 0, xc_buf[j])

    def d_core(j):
        if j in ZLAST:
            zg_wait("hz", j, 4)
        else:
            g4_done("hx", j)
        send(("core", j), xh[j].at[c], xh[j].at[c], dev_sib)

    def d_hotmm(j):
        got(("core", j))
        weights_in()
        gate_up(j, 1, xh[j].at[0])
        gate_up(j, 2, xh[j].at[1])

    def activate(block, masked):
        @pl.loop(0, 8, unroll=True)
        def _(i):
            rows = pl.ds(pl.multiple_of(i * 64, 64), 64)
            gate = acc[block, rows, 0:384]
            up = acc[block, rows, 384:768]
            value = gate / (1.0 + jnp.exp(-gate)) * up
            if masked:
                value = jnp.where(hot_ref[0:1, 0:1] > 0.5, value, 0.0)
            act[block, rows, :] = value.astype(BF)

    def down(j, block, at, shape):
        @pl.loop(0, WIDTHS[j] // 256, unroll=True)
        def _(n):
            cols = pl.ds(pl.multiple_of(n * 256, 256), 256)
            wcols = pl.ds(pl.multiple_of(OFFS[j] + n * 256, 256), 256)
            part = jnp.dot(act[block], wd[:, wcols], preferred_element_type=F32)
            at[(slice(None),) * len(shape) + (cols,)] = part.astype(BF).reshape(shape + (256,))

    def silu_cold(j):
        loads[2].wait()
        activate(0, False)

    def silu_hot(j):
        activate(1, True)
        activate(2, True)

    def ry_at(j):
        return lambda k: ry[j].at[k]

    def rx_at(j):
        if j in ZLAST:
            return lambda k: rx[j].at[k]
        return lambda k: rx[j].at[k]

    def rh_at(j):
        if j in ZLAST:
            return lambda k: rh[j].at[k]
        return lambda k: rh[j].at[k]

    def e_down(j):
        sent(lambda key: key[0] == "cy" and key[1] == j)
        down(j, 0, xc_buf[j], (4, 8, 16))
        r4_first("ry", j, cold_at(j), ry_at(j), y, dev_y)

    def e_second(j):
        r4_second("ry", j, cold_at(j), ry_at(j), y, dev_y)

    def e_return(j):
        r4_done("ry", j, cold_at(j), ry_at(j), y)
        for k in range(1, 8):
            send(("back", j, k), xc_buf[j].at[y, lax.rem(xcore + k, 8)], rr[j].at[xcore], dev_xc(k))
        rr[j][xcore] = xc_buf[j][y, xcore]

    def f_down(j):
        sent(lambda key: key[0] in ("hy", "hx", "hz", "core") and key[1] == j)
        down(j, 1, xh[j].at[0], (4, 4, 2, 16))
        down(j, 2, xh[j].at[1], (4, 4, 2, 16))
        send(("hcore", j), xh[j].at[1 - c], hc[j], dev_sib)

    def core_sum(j):
        got(("hcore", j))
        for i in range(4):
            tiles(xh[j].at[c, i], xh[j].at[c, i], hc[j].at[i])

    def ring_send(tag, j, s, block, slot):
        plus, minus = hops(j)
        if s <= plus:
            send((tag, j, "p", s), block(add(z, plus - s + 1, NZ)), slot(s - 1), dev_z(1))
        if s <= minus:
            send((tag, j, "m", s), block(add(z, -(minus - s + 1), NZ)), slot(plus + s - 1), dev_z(-1))

    def ring_sum(tag, j, s, block, slot):
        plus, minus = hops(j)
        if s - 1 <= plus:
            got((tag, j, "p", s - 1))
            if s <= plus:
                b = add(z, plus - s + 1, NZ)
                summed(block(b), block(b), slot(s - 2))
        if s - 1 <= minus:
            got((tag, j, "m", s - 1))
            if s <= minus:
                b = add(z, -(minus - s + 1), NZ)
                summed(block(b), block(b), slot(plus + s - 2))

    def zh_at(j):
        return lambda k: zh[ZLAST.index(j)].at[k]

    def f_z(s, j):
        if s == 1:
            core_sum(j)
        else:
            ring_sum("fz", j, s, slice_at(j), zh_at(j))
        ring_send("fz", j, s, slice_at(j), zh_at(j))

    def f_x1(j):
        if j in ZLAST:
            ring_sum("fz", j, 5, slice_at(j), zh_at(j))
            mine = slice_at(j)(z)
            summed(mine, mine, zh_at(j)(hops(j)[0] - 1), zh_at(j)(6))
            d4_reduce("rx", j, hotx_at(j), rx_at(j), x, dev_x)
        else:
            core_sum(j)
            r4_first("rx", j, hotx_at(j), rx_at(j), x, dev_x)

    def f_x2(j):
        r4_second("rx", j, hotx_at(j), rx_at(j), x, dev_x)

    def f_y1(j):
        if j in ZLAST:
            d4_sum("rx", j, hotx_at(j), rx_at(j), x)
            d4_reduce("rh", j, hoty_at(j), rh_at(j), y, dev_y)
        else:
            r4_done("rx", j, hotx_at(j), rx_at(j), x)
            r4_first("rh", j, hoty_at(j), rh_at(j), y, dev_y)

    def f_y2(j):
        r4_second("rh", j, hoty_at(j), rh_at(j), y, dev_y)

    def f_done(j):
        if j in ZLAST:
            d4_sum("rh", j, hoty_at(j), rh_at(j), y)
        else:
            r4_done("rh", j, hoty_at(j), rh_at(j), y)

    def tk_at(j):
        return lambda k: tk[j].at[k]

    def zr_at(j):
        return lambda k: zr[j].at[k]

    def g_combine(j):
        for k in range(1, 8):
            got(("back", j, k))

        @pl.loop(0, WIDTHS[j] // 256, unroll=True)
        def _(n):
            cols = pl.ds(pl.multiple_of(n * 256, 256), 256)
            cold = rr[j][:, :, cols].reshape(128, 256)
            total = jnp.dot(mcomb[0], cold, preferred_element_type=F32)
            total += jnp.dot(mcomb[1], cold, preferred_element_type=F32)
            if j not in ZLAST:
                total += hot_part(xh[j][c, x, y, :, :, cols].reshape(32, 256))
            tk[j][:, :, cols] = total.astype(BF).reshape(8, 16, 256)

        if j in ZLAST:
            cold = rr[j][:, :, part_of(j, z)].reshape(128, WIDTHS[j] // NZ)
            total = jnp.dot(mcomb[0], cold, preferred_element_type=F32)
            total += jnp.dot(mcomb[1], cold, preferred_element_type=F32)
            total += hot_part(xh[j][c, x, y, :, :, part_of(j, z)].reshape(32, WIDTHS[j] // NZ))
            tk[j][:, :, part_of(j, z)] = total.astype(BF).reshape(8, 16, WIDTHS[j] // NZ)
        if j in RDIR:
            for k in (4, 1, 7, 2, 6, 3, 5):
                send(("rz", j, k), tk[j].at[add(z, k, NZ)], zr[j].at[k - 1], dev_z(k))
        else:
            ring_send("rz", j, 1, tk_at(j), zr_at(j))

    def hot_part(rows):
        total = jnp.dot(mcomb[2][:, 0:32], rows, preferred_element_type=F32)
        return total + jnp.dot(mcomb[3][:, 0:32], rows, preferred_element_type=F32)

    def g_step(s, j):
        ring_sum("rz", j, s, tk_at(j), zr_at(j))
        ring_send("rz", j, s, tk_at(j), zr_at(j))

    def g_out(j):
        if j in RDIR:
            for k in range(1, NZ):
                got(("rz", j, k))
            summed(out_ref.at[:, pl.ds(OFFS[j], WIDTHS[j])], tk[j].at[z], *[zr[j].at[k] for k in range(7)])
            return
        ring_sum("rz", j, 5, tk_at(j), zr_at(j))
        summed(out_ref.at[:, pl.ds(OFFS[j], WIDTHS[j])], tk[j].at[z], zr[j].at[hops(j)[0] - 1], zr[j].at[6])

    def stepped(f):
        return [functools.partial(f, s) for s in range(1, 5)]

    steps = {
        "z1": d_zstart, "selc": d_pickcold, "selh": d_pickhot, "hy2": d_hoty2, "hx1": d_hotx1, "hx2": d_hotx2, "core": d_core,
        "cy1": d_coldy1, "cy2": d_coldy2, "cmm": d_coldmm, "hmm": d_hotmm, "silc": silu_cold,
        "silh": silu_hot, "edn": e_down, "e2": e_second, "ret": e_return, "fdn": f_down, "fx1": f_x1,
        "fx2": f_x2, "fy1": f_y1, "fy2": f_y2, "fdone": f_done, "comb": g_combine, "out": g_out,
    }
    for name, f in (("z", d_zstep), ("hz", d_hotz), ("fz", f_z), ("gz", g_step)):
        for s, g in enumerate(stepped(f), 1):
            steps.setdefault(name + str(s), g)
    for name, j in ORDER:
        steps[name](j)
    sent(lambda key: True)


def local(hidden_states, expert_ids, route_weights, w_gate, w_up, w_down):
    rows, width = hidden_states.shape
    vmem = pl.BlockSpec(memory_space=pltpu.VMEM)
    hbm = pl.BlockSpec(memory_space=pl.ANY)

    def each(*shape):
        return [pltpu.VMEM(shape + (w,), BF) for w in WIDTHS]

    def slots(full, part):
        return [pltpu.VMEM(part + (w // NZ,) if j in ZLAST else full + (w,), BF) for j, w in enumerate(WIDTHS)]

    scratch = [
        each(8, 16),
        pltpu.VMEM((8, 16, 128), F32),
        each(10, 16),
        each(4, 8, 16),
        each(2, 4, 4, 2, 16),
        pltpu.VMEM((width, 768), BF),
        pltpu.VMEM((384, width), BF),
        pltpu.VMEM((3, 512, 768), F32),
        pltpu.VMEM((3, 512, 384), BF),
        each(6, 4, 16),
        each(4, 4, 2, 16),
        slots((6, 2, 2, 16), (3, 4, 2, 16)),
        slots((6, 16), (3, 2, 16)),
        each(8, 16),
        each(8, 16),
        each(7, 16),
        [pltpu.VMEM((7, 4, 4, 2, 16, WIDTHS[j] // NZ), BF) for j in ZLAST],
        pltpu.VMEM((8, 128), F32),
        pltpu.VMEM((160, 128), BF),
        pltpu.VMEM((4, 128, 128), BF),
        pltpu.SemaphoreType.DMA((CHUNKS * NSEM + 8,)),
        pltpu.SemaphoreType.DMA((CHUNKS * NSEM + 8,)),
        pltpu.SemaphoreType.DMA((3,)),
    ]
    return pl.pallas_call(
        kernel,
        out_shape=jax.ShapeDtypeStruct((rows, width), BF),
        in_specs=[vmem, vmem, vmem, hbm, hbm, hbm],
        out_specs=vmem,
        scratch_shapes=scratch,
        compiler_params=pltpu.CompilerParams(
            collective_id=0, has_side_effects=True, vmem_limit_bytes=60 * 1024 * 1024),
    )(hidden_states, expert_ids.T, route_weights.T, w_gate, w_up, w_down)


def solution(mesh):
    in_specs = (
        P(("rep", "exp"), None),
        P(("rep", "exp"), None),
        P(("rep", "exp"), None),
        P("exp", None, "rep"),
        P("exp", None, "rep"),
        P("exp", "rep", None),
    )
    out_specs = P(("rep", "exp"), None)
    return jax.shard_map(local, mesh=mesh, in_specs=in_specs, out_specs=out_specs, check_vma=False)
```
